32 devices in a mesh: dp: 8 (over y, x, core), seq: 4 (over z).
Axes of the slice: x: 2, y: 2, z: 4, core: 2. Of those that a mesh axis runs over, the one named last changes fastest.
Arguments:
- query: bfloat16 [8192, 1536], P(('dp', 'seq')), parts along dimension 0
- keys: bfloat16 [8192, 1536], P(('dp', 'seq')), parts along dimension 0
- values: bfloat16 [8192, 1536], P(('dp', 'seq')), parts along dimension 0, may hold values from -6 to 6
- adjacency: int32 [8192, 8], P(('dp', 'seq')), parts along dimension 0, may hold values from 0 to 1023, as said below
- tissue: int32 [8192], P(('dp', 'seq')), parts along dimension 0, may hold values from 0 to 1, as said below
- offsets: int32 [12], replicated, may hold values from 0 to 1, as said below
- local_bias: float32 [12], replicated, may hold values from 3 to 7
- w_out: bfloat16 [1536, 1536], replicated, may hold values from -0.15625 to 0.15625
- teacher_tile: bfloat16 [8192, 1536], P(('dp', 'seq')), parts along dimension 0, may hold values from -6 to 6
- teacher_slide: float32 [12288], P('dp'), parts along dimension 0, may hold values from -6 to 6
Outputs:
- tile_embed: bfloat16 [8192, 1536], P(('dp', 'seq')), parts along dimension 0
- tile_loss: float32 [8192], P(('dp', 'seq')), parts along dimension 0
- slide_embed: float32 [12288], P('dp'), parts along dimension 0
- loss: float32 [8], P('dp'), parts along dimension 0
The draws below stay inside these ranges and needn't reach their ends.
There are 8 independent parts, one for each index of `dp`. The reference program is written for one: setup_inputs(seed, part) draws one part's arguments, and reference() takes and returns one part's arrays. A program takes and returns all parts, laid end to end along the dimension named above; an argument that names none is the same for every part. Nothing has to cross between parts.
Inputs may be any that keep to these rules, and one draw needn't show every extreme that they name: `adjacency`: every entry is a tile of the same slide whose position differs from the row's tile by at most 32. `tissue`: constant over aligned blocks of 16 tiles; the 256 tiles of each index of seq hold at least one block of ones. `offsets`: every value from 0 to 1 is the offset of some head.
All inputs are finite; a program needn't handle non-finite values.
Results may differ from the reference program's by a relative error of at most 0.0085.
Values may be sent and summed in bfloat16 or wider, within the bound.
No kernel may reach another device: no remote copies, remote signals or barrier semaphores. Data moves between devices by JAX's collectives and lax.ppermute only.
A program may use at most 192 MiB of HBM per device.

```python
import math
import jax
import jax.numpy as jnp
from jax import lax

ATTENTION_HEADS = 12
HEAD_SIZE = 128
D = 1536
NBR = 8
NEIGHBOUR_REACH = 32
DILATION_STEP = 2
MB = 16
TPD = 256
SLIDE_TILES = 1024


def make_adjacency(key):
    moves = jax.random.randint(jax.random.fold_in(key, 11), (SLIDE_TILES, NBR), -NEIGHBOUR_REACH, NEIGHBOUR_REACH + 1, dtype=jnp.int32)
    places = jnp.arange(SLIDE_TILES, dtype=jnp.int32)[:, None]
    return jnp.clip(places + moves, 0, SLIDE_TILES - 1).astype(jnp.int32)


def make_pairs(key):
    query = jax.random.normal(jax.random.fold_in(key, 31), (SLIDE_TILES, D), jnp.float32)
    keys = jax.random.normal(jax.random.fold_in(key, 32), (SLIDE_TILES, D), jnp.float32)
    return (query, keys)


def draw_query(key, part):
    return make_pairs(key)[0].astype(jnp.bfloat16)


def draw_keys(key, part):
    return make_pairs(key)[1].astype(jnp.bfloat16)


def draw_adjacency(key, part):
    return make_adjacency(key)


def draw_tissue(key, part):
    blocks_device = TPD // MB
    device_count = SLIDE_TILES // TPD
    block_count = SLIDE_TILES // MB
    owner = jnp.arange(block_count, dtype=jnp.int32) // blocks_device
    limit = 250 + 650 * owner // max(device_count - 1, 1)
    rolled = jax.random.randint(jax.random.fold_in(key, 22), (block_count,), 0, 1000, dtype=jnp.int32)
    picked = jax.random.randint(jax.random.fold_in(key, 23), (device_count,), 0, blocks_device, dtype=jnp.int32)
    forced = jnp.arange(block_count, dtype=jnp.int32) % blocks_device == picked[owner]
    kept = jnp.logical_or(rolled < limit, forced).astype(jnp.int32)
    return jnp.repeat(kept, MB).astype(jnp.int32)


def draw_offsets(key, part):
    return (jax.random.permutation(jax.random.fold_in(key, 44), ATTENTION_HEADS) % DILATION_STEP).astype(jnp.int32)


def levels(stream_key, dims, pieces, smallest, high):
    level, own = 1.0, jax.random.fold_in(stream_key, 6)
    for axis_at, blocks in pieces:
        heights = jnp.exp(jax.random.uniform(jax.random.fold_in(own, axis_at), (blocks,), jnp.float32, smallest / len(pieces), high / len(pieces)))
        level = level * jnp.repeat(heights, dims[axis_at] // blocks).reshape([-1 if axis == axis_at else 1 for axis in range(len(dims))])
    return level


def scatter_about(rng, shape, width, most, cuts=(), kind=jnp.bfloat16):
    entries = jax.random.normal(rng, shape, jnp.float32) * width
    if len(cuts) > 0:
        entries = levels(rng, shape, cuts, -0.22, 0.18) * entries
    return jnp.clip(entries, min=-most, max=most).astype(kind)


def setup_inputs(seed: int = 0, part: int = 0) -> dict:
    key_list = jax.random.split(jax.random.key(seed), 11)
    part_splits = jax.random.split(jax.random.fold_in(key_list[10], part), 11)
    query = draw_query(jax.random.fold_in(jax.random.fold_in(key_list[10], part), 71), part)
    keys = draw_keys(jax.random.fold_in(jax.random.fold_in(key_list[10], part), 71), part)
    values = scatter_about(part_splits[2], (SLIDE_TILES, D), 1.0, 6.0, ((0, 4),))
    adjacency = draw_adjacency(jax.random.fold_in(jax.random.fold_in(key_list[10], part), 71), part)
    tissue = draw_tissue(jax.random.fold_in(jax.random.fold_in(key_list[10], part), 71), part)
    offsets = draw_offsets(jax.random.fold_in(key_list[10], 71), part)
    local_bias = jnp.clip(jax.random.uniform(key_list[6], (ATTENTION_HEADS,), jnp.float32, 3.0, 7.0), 3.0, 7.0)
    w_out = scatter_about(key_list[7], (D, D), D ** -0.5, 0.15625)
    teacher_tile = scatter_about(part_splits[8], (SLIDE_TILES, D), 1.0, 6.0, ((0, 4),))
    teacher_slide = scatter_about(part_splits[9], (D,), 1.0, 6.0, (), jnp.float32)
    return dict(query=query, keys=keys, values=values, adjacency=adjacency, tissue=tissue, offsets=offsets, local_bias=local_bias, w_out=w_out, teacher_tile=teacher_tile, teacher_slide=teacher_slide)


def layer_norm(inputs):
    centred = inputs - lax.optimization_barrier(jnp.mean(inputs, axis=-1, keepdims=True))
    return centred * lax.rsqrt(lax.optimization_barrier(jnp.mean(centred * centred, axis=-1, keepdims=True)) + 1e-05)

def cosine(first, second):
    inner = lax.optimization_barrier(jnp.mean(first * second, axis=-1))
    return inner * lax.rsqrt(lax.optimization_barrier(jnp.mean(first * first, axis=-1)) + 1e-06) * lax.rsqrt(lax.optimization_barrier(jnp.mean(second * second, axis=-1)) + 1e-06)

def reference(query, keys, values, adjacency, tissue, offsets, local_bias, w_out, teacher_tile, teacher_slide):
    score_scale = 1.0 / math.sqrt(HEAD_SIZE)
    queries = query.astype(jnp.float32).reshape(SLIDE_TILES, ATTENTION_HEADS, HEAD_SIZE)
    key_matrix_rows = keys.astype(jnp.float32).reshape(SLIDE_TILES, ATTENTION_HEADS, HEAD_SIZE)
    value_matrix_rows = values.astype(jnp.float32).reshape(SLIDE_TILES, ATTENTION_HEADS, HEAD_SIZE)
    selected_rows = offsets[None, :] == jnp.arange(DILATION_STEP, dtype=jnp.int32)[:, None]
    distant_keys = lax.optimization_barrier(jnp.sum(jnp.where(selected_rows[None, :, :, None], key_matrix_rows.reshape(SLIDE_TILES // DILATION_STEP, DILATION_STEP, ATTENTION_HEADS, HEAD_SIZE), 0.0), axis=1))
    distant_values = lax.optimization_barrier(jnp.sum(jnp.where(selected_rows[None, :, :, None], value_matrix_rows.reshape(SLIDE_TILES // DILATION_STEP, DILATION_STEP, ATTENTION_HEADS, HEAD_SIZE), 0.0), axis=1))
    distant_mask = lax.optimization_barrier(jnp.sum(jnp.where(selected_rows[None], tissue.reshape(SLIDE_TILES // DILATION_STEP, DILATION_STEP)[:, :, None], 0), axis=1)) > 0
    listing = jnp.concatenate([jnp.arange(SLIDE_TILES, dtype=jnp.int32)[:, None], adjacency.astype(jnp.int32)], axis=1)
    block_rows = math.gcd(SLIDE_TILES, 512)

    def one_block(start):
        block_queries = lax.dynamic_slice_in_dim(queries, start, block_rows, 0)
        block_list = lax.dynamic_slice_in_dim(listing, start, block_rows, 0)
        near_keys = key_matrix_rows[block_list]
        near_values = value_matrix_rows[block_list]
        near_scores = jnp.einsum('the,tnhe->thn', block_queries, near_keys) * score_scale + local_bias[None, :, None]
        far_scores = jnp.einsum('the,rhe->thr', block_queries, distant_keys) * score_scale
        far_scores = jnp.where(distant_mask.T[None], far_scores, -jnp.inf)
        top = jnp.maximum(lax.optimization_barrier(jnp.max(near_scores, axis=-1)), lax.optimization_barrier(jnp.max(far_scores, axis=-1)))
        near_weights = jnp.exp(near_scores - top[..., None])
        far_weights = jnp.exp(far_scores - top[..., None])
        total = lax.optimization_barrier(jnp.sum(near_weights, axis=-1)) + lax.optimization_barrier(jnp.sum(far_weights, axis=-1))
        mixed = jnp.einsum('thn,tnhe->the', near_weights.astype(jnp.bfloat16).astype(jnp.float32), near_values)
        mixed = mixed + jnp.einsum('thr,rhe->the', far_weights.astype(jnp.bfloat16).astype(jnp.float32), distant_values)
        return (mixed / total[..., None]).astype(jnp.bfloat16).reshape(block_rows, ATTENTION_HEADS * HEAD_SIZE)
    starts = jnp.arange(SLIDE_TILES // block_rows, dtype=jnp.int32) * block_rows
    attended = lax.map(one_block, starts).reshape(SLIDE_TILES, ATTENTION_HEADS * HEAD_SIZE)
    projected = jnp.dot(attended, w_out, preferred_element_type=jnp.float32)
    embedding = layer_norm(projected)
    valid_mask = tissue.astype(jnp.float32)
    pooled = lax.optimization_barrier(jnp.sum(embedding * valid_mask[:, None], axis=0))
    slide_embed = layer_norm(pooled)
    tile_loss = 1.0 - cosine(embedding, teacher_tile.astype(jnp.float32))
    distance = jnp.sum(tile_loss * valid_mask)
    loss = distance / jnp.sum(valid_mask) + 1.0 - cosine(slide_embed, teacher_slide)
    return (embedding.astype(jnp.bfloat16), tile_loss, slide_embed, loss.reshape(1))
```

```python
import functools
import math

import jax
import jax.numpy as jnp
from jax import lax
from jax.experimental import pallas as pl
from jax.experimental.pallas import tpu as pltpu
from jax.sharding import PartitionSpec as P

REACH = 32
STEP = 2
MASK_BLOCK = 16
HEAD = 128
GROUPS = (4, 4, 4)
MARK = 64.0
LOG2E = math.log2(math.e)
F32 = jnp.float32
BF16 = jnp.bfloat16
VMEM = pl.BlockSpec(memory_space=pltpu.VMEM)
SMEM = pl.BlockSpec(memory_space=pltpu.SMEM)


def nt(a, b):
    return lax.dot_general(a, b, (((1,), (1,)), ((), ())), preferred_element_type=F32)


def tn(a, b):
    return lax.dot_general(a, b, (((0,), (0,)), ((), ())), preferred_element_type=F32)


def call(body, outs, flops, size, limit=32):
    return functools.partial(
        pl.pallas_call,
        body,
        out_shape=outs,
        compiler_params=pltpu.CompilerParams(vmem_limit_bytes=limit * 1024 * 1024),
        cost_estimate=pl.CostEstimate(flops=flops, bytes_accessed=size, transcendentals=0),
    )


def tissue_rows(tissue_ref, rows_per_block, blocks):
    return jnp.concatenate(
        [
            jnp.full((rows_per_block, HEAD), tissue_ref[b * MASK_BLOCK], jnp.int32)
            for b in range(blocks)
        ],
        axis=0,
    )


def pack_kernel(groups, offsets_ref, tissue_ref, q_ref, k_ref, v_ref, *out_refs):
    count = len(groups)
    kv_refs, q_refs = out_refs[:count], out_refs[count : 2 * count]
    low_ref, high_ref = out_refs[2 * count :]
    tiles = k_ref.shape[0]
    pairs = tiles // STEP
    low_ref[:REACH] = k_ref[:REACH]
    low_ref[REACH:] = v_ref[:REACH]
    high_ref[:REACH] = k_ref[tiles - REACH :]
    high_ref[REACH:] = v_ref[tiles - REACH :]
    rows = lax.broadcasted_iota(jnp.int32, (pairs, tiles), 0) * STEP
    cols = lax.broadcasted_iota(jnp.int32, (pairs, tiles), 1)
    keep = tissue_rows(tissue_ref, MASK_BLOCK // STEP, tiles // MASK_BLOCK) > 0
    head = 0
    for group, size in enumerate(groups):
        width = size * HEAD
        q_refs[group][...] = q_ref[:, head * HEAD : head * HEAD + width]
        for local in range(size):
            at = slice((head + local) * HEAD, (head + local + 1) * HEAD)
            pick = jnp.where(cols == rows + offsets_ref[head + local], 1.0, 0.0).astype(BF16)
            key = jnp.dot(pick, k_ref[:, at], preferred_element_type=F32)
            value = jnp.dot(pick, v_ref[:, at], preferred_element_type=F32)
            lane = local * HEAD
            kv_refs[group][:, lane : lane + HEAD] = key.astype(BF16)
            kv_refs[group][:, width + lane : width + lane + HEAD] = jnp.where(
                keep, value, MARK
            ).astype(BF16)
        head += size


def mark_bias(values):
    return jnp.where(values.astype(F32) > 0.5 * MARK, -jnp.inf, 0.0)


def split3(x):
    high = x.astype(BF16).astype(F32)
    rest = x - high
    mid = rest.astype(BF16).astype(F32)
    return high, mid, rest - mid


def softmax_rows(scores, values):
    top = jnp.max(scores, axis=0, keepdims=True)
    weights = jnp.exp2(scores - top)
    total = jnp.sum(weights, axis=0, keepdims=True)
    mixed = tn(values, weights.astype(BF16))
    return mixed / total, top + jnp.log2(total)


def near_kernel(groups, scale, *refs):
    count = len(groups)
    bias_ref, base_ref, q_ref, k_ref, v_ref = refs[:5]
    kv_refs = refs[5 : 5 + count]
    left_ref, right_ref, adj_ref, out_ref, lse_ref = refs[5 + count :]
    tiles = k_ref.shape[0]
    half = tiles // 2
    window = half + 2 * REACH
    base = base_ref[0]
    mark = mark_bias(kv_refs[0][:, groups[0] * HEAD : (groups[0] + 1) * HEAD])
    counts = []
    spot = lax.broadcasted_iota(jnp.int32, (window, half), 0)
    lane = lax.broadcasted_iota(jnp.int32, (window, half), 1)
    for part in range(2):
        place = spot + (base - REACH + part * half)
        number = jnp.where(spot == lane + REACH, 1.0, 0.0)
        for entry in range(adj_ref.shape[0]):
            listed = adj_ref[entry : entry + 1, part * half : (part + 1) * half]
            number = number + jnp.where(place == listed, 1.0, 0.0)
        counts.append(number)
    row = lax.broadcasted_iota(jnp.int32, (16, half), 0)
    lses = [jnp.zeros((16, half), F32) for _ in range(2)]
    head = 0
    for group, size in enumerate(groups):
        for local in range(size):
            at = slice(head * HEAD, (head + 1) * HEAD)
            far_key = kv_refs[group][:, local * HEAD : (local + 1) * HEAD]
            far_value = kv_refs[group][:, (size + local) * HEAD : (size + local + 1) * HEAD]
            shift = bias_ref[head] * LOG2E
            for part in range(2):
                q = q_ref[part * half : (part + 1) * half, at]
                if part == 0:
                    cut = slice(0, half + REACH)
                    key = jnp.concatenate([left_ref[:REACH, at], k_ref[cut, at]], axis=0)
                    value = jnp.concatenate([left_ref[REACH:, at], v_ref[cut, at]], axis=0)
                else:
                    cut = slice(half - REACH, tiles)
                    key = jnp.concatenate([k_ref[cut, at], right_ref[:REACH, at]], axis=0)
                    value = jnp.concatenate([v_ref[cut, at], right_ref[REACH:, at]], axis=0)
                far = nt(far_key, q) * scale + mark
                near = nt(key, q) * scale + shift
                near = jnp.where(counts[part] > 0, near, -jnp.inf)
                top = jnp.maximum(
                    jnp.max(far, axis=0, keepdims=True), jnp.max(near, axis=0, keepdims=True)
                )
                far = jnp.exp2(far - top)
                near = jnp.exp2(near - top) * counts[part]
                total = jnp.sum(far, axis=0, keepdims=True) + jnp.sum(near, axis=0, keepdims=True)
                mixed = tn(far_value, far.astype(BF16)) + tn(value, near.astype(BF16))
                out_ref[at, part * half : (part + 1) * half] = (mixed / total).astype(BF16)
                lses[part] = jnp.where(row == head, top + jnp.log2(total), lses[part])
            head += 1
    for part in range(2):
        lse_ref[:, part * half : (part + 1) * half] = lses[part]


def far_heads(q_ref, kv_refs, size, scale, chosen=None):
    width = size * HEAD
    tiles = q_ref.shape[0]

    def read(number, at):
        return kv_refs[number][at] if chosen is None else chosen(number, at)

    marks = jnp.concatenate(
        [
            mark_bias(read(n, (slice(None), slice(width, width + HEAD))))
            for n in range(len(kv_refs))
        ],
        axis=0,
    )
    marks = jnp.concatenate([marks] * (tiles // HEAD), axis=1)
    for local in range(size):
        at = (slice(None), slice(local * HEAD, (local + 1) * HEAD))
        vat = (slice(None), slice(width + local * HEAD, width + (local + 1) * HEAD))
        key = jnp.concatenate([read(n, at) for n in range(len(kv_refs))], axis=0)
        value = jnp.concatenate([read(n, vat) for n in range(len(kv_refs))], axis=0)
        scores = nt(key, q_ref[at]) * scale + marks
        yield local, *softmax_rows(scores, value)


def guest_kernel(size, scale, active_ref, q_ref, a_ref, b_ref, c_ref, out_ref):
    width = size * HEAD

    @pl.when(active_ref[0] > 0)
    def _():
        row = lax.broadcasted_iota(jnp.int32, (16, q_ref.shape[0]), 0)
        stats = jnp.zeros((16, q_ref.shape[0]), F32)
        for local, mixed, lse in far_heads(q_ref, (a_ref, b_ref, c_ref), size, scale):
            out_ref[local * HEAD : (local + 1) * HEAD] = mixed.astype(BF16)
            for piece, term in enumerate(split3(lse)):
                stats = jnp.where(row == 3 * local + piece, term, stats)
        out_ref[width:] = stats.astype(BF16)


def far_kernel(groups, shards, scale, active_ref, *refs):
    count = len(groups)
    q_refs, kv_refs = refs[:count], refs[count : count * (1 + shards)]
    out_ref, lse_ref = refs[count * (1 + shards) :]

    @pl.when(active_ref[0] > 0)
    def _():
        tiles = q_refs[0].shape[0]
        row = lax.broadcasted_iota(jnp.int32, (16, tiles), 0)
        lses = jnp.zeros((16, tiles), F32)
        head = 0
        for group, size in enumerate(groups):
            parts = kv_refs[group * shards : (group + 1) * shards]
            for local, mixed, lse in far_heads(q_refs[group], parts, size, scale):
                out_ref[(head + local) * HEAD : (head + local + 1) * HEAD] = mixed.astype(BF16)
                lses = jnp.where(row == head + local, lse, lses)
            head += size
        lse_ref[...] = lses


def ring_kernel(size, scale, order_ref, q_ref, kv_ref, out_ref, lse_ref):
    shards = kv_ref.shape[0] - 1
    tiles = q_ref.shape[0]
    row = lax.broadcasted_iota(jnp.int32, (16, tiles), 0)
    lses = jnp.zeros((16, tiles), F32)
    refs = [kv_ref] * shards

    def chosen(number, at):
        return kv_ref[(order_ref[number],) + at]

    for local, mixed, lse in far_heads(q_ref, refs, size, scale, chosen):
        out_ref[local * HEAD : (local + 1) * HEAD] = mixed.astype(BF16)
        lses = jnp.where(row == local, lse, lses)
    lse_ref[...] = lses


def final_kernel(groups, *refs):
    message_count = len(refs) - 13
    active_ref, tissue_ref, near_ref, near_lse_ref, far_ref, far_lse_ref = refs[:6]
    messages = refs[6 : 6 + message_count]
    w_ref, teacher_ref, embed_ref, loss_ref, sums_ref, att_ref = refs[6 + message_count : -1]
    (proj_ref,) = refs[-1:]
    tiles, width = teacher_ref.shape

    def merge(head, other, other_lse):
        at = slice(head * HEAD, (head + 1) * HEAD)
        own_lse = near_lse_ref[head : head + 1]
        top = jnp.maximum(own_lse, other_lse)
        own = jnp.exp2(own_lse - top)
        rest = jnp.exp2(other_lse - top)
        inverse = 1.0 / (own + rest)
        att_ref[at] = (
            near_ref[at].astype(F32) * (own * inverse) + other.astype(F32) * (rest * inverse)
        ).astype(BF16)

    def from_far():
        for head in range(sum(groups)):
            merge(head, far_ref[head * HEAD : (head + 1) * HEAD], far_lse_ref[head : head + 1])

    if message_count == 0:
        from_far()
    else:
        pl.when(active_ref[0] > 0)(from_far)

        @pl.when(active_ref[0] == 0)
        def _():
            head = 0
            for group, size in enumerate(groups):
                stats = messages[group][size * HEAD :].astype(F32)
                for local in range(size):
                    at = 3 * local
                    lse = stats[at : at + 1] + stats[at + 1 : at + 2] + stats[at + 2 : at + 3]
                    merge(head, messages[group][local * HEAD : (local + 1) * HEAD], lse)
                    head += 1

    proj_ref[...] = tn(att_ref[...], w_ref[...])
    scale = 1.0 / width
    proj = proj_ref[...]
    centred = proj - jnp.sum(proj, axis=1, keepdims=True) * scale
    square = jnp.sum(centred * centred, axis=1, keepdims=True) * scale
    embed = centred * lax.rsqrt(square + 1e-05)
    embed_ref[...] = embed.astype(BF16)
    teacher = teacher_ref[...].astype(F32)
    inner = jnp.sum(embed * teacher, axis=1, keepdims=True) * scale
    first = jnp.sum(embed * embed, axis=1, keepdims=True) * scale
    second = jnp.sum(teacher * teacher, axis=1, keepdims=True) * scale
    loss = 1.0 - inner * lax.rsqrt(first + 1e-06) * lax.rsqrt(second + 1e-06)
    loss_ref[...] = jnp.transpose(jnp.broadcast_to(loss, (tiles, HEAD)))[:1]
    marks = tissue_rows(tissue_ref, MASK_BLOCK, tiles // MASK_BLOCK).astype(F32)[:, :1]
    pooled = jnp.sum(embed * marks, axis=0, keepdims=True)
    row = lax.broadcasted_iota(jnp.int32, (16, HEAD), 0)
    lane = lax.broadcasted_iota(jnp.int32, (16, HEAD), 1)
    blocks = width // HEAD
    sums = jnp.where(lane == 0, jnp.sum(loss * marks), jnp.sum(marks))
    for block in range(blocks):
        sums = jnp.where(row == block, pooled[:, block * HEAD : (block + 1) * HEAD], sums)
    sums_ref[...] = sums


def slide_kernel(first_ref, second_ref, teacher_ref, slide_ref, loss_ref):
    total = first_ref[...] + second_ref[...]
    blocks = teacher_ref.shape[0]
    scale = 1.0 / (blocks * HEAD)
    pooled = total[:blocks]

    def mean(x):
        return jnp.sum(jnp.sum(x, axis=0, keepdims=True), axis=1, keepdims=True) * scale

    centred = pooled - mean(pooled)
    slide = centred * lax.rsqrt(mean(centred * centred) + 1e-05)
    slide_ref[...] = slide
    teacher = teacher_ref[...]
    cosine = (
        mean(slide * teacher)
        * lax.rsqrt(mean(slide * slide) + 1e-06)
        * lax.rsqrt(mean(teacher * teacher) + 1e-06)
    )
    distance = total[blocks : blocks + 1, 0:1]
    number = total[blocks : blocks + 1, 1:2]
    loss_ref[0] = jnp.sum(distance / number + 1.0 - cosine)


def sds(shape, dtype):
    return jax.ShapeDtypeStruct(shape, dtype)


def per_device(
    query, keys, values, adjacency, tissue, offsets, local_bias, w_out, teacher_tile, teacher_slide
):
    tiles, width = query.shape
    heads = offsets.shape[0]
    pairs = tiles // STEP
    groups = GROUPS
    scale = LOG2E / math.sqrt(HEAD)
    ring = lax.axis_size("seq")
    place = lax.axis_index("seq")

    def move(x, route):
        return lax.ppermute(x, "seq", route)

    rightward = [(i, i + 1) for i in range(ring - 1)]
    leftward = [(i + 1, i) for i in range(ring - 1)]

    kv_shapes = [sds((pairs, 2 * size * HEAD), BF16) for size in groups]
    q_shapes = [sds((tiles, size * HEAD), BF16) for size in groups]
    edge = sds((2 * REACH, width), BF16)
    packed = call(
        functools.partial(pack_kernel, groups),
        tuple(kv_shapes + q_shapes + [edge, edge]),
        4 * pairs * tiles * width,
        5 * tiles * width * 2,
    )(in_specs=[SMEM, SMEM, VMEM, VMEM, VMEM])(offsets, tissue, query, keys, values)
    count = len(groups)
    kv, q, (low, high) = packed[:count], packed[count : 2 * count], packed[2 * count :]

    inner = ring == 4
    if inner:
        active = jnp.logical_and(place > 0, place < 3).astype(jnp.int32).reshape(1)
        from_left = [move(x, [(0, 1), (1, 2)]) for x in kv]
        from_right = [move(x, [(3, 2), (2, 1)]) for x in kv]
        guest_q = [move(x, [(0, 1), (3, 2)]) for x in q]
    left = move(high, rightward)
    right = move(low, leftward)

    base = (place * tiles).astype(jnp.int32).reshape(1)
    near, near_lse = call(
        functools.partial(near_kernel, groups, scale),
        (sds((width, tiles), BF16), sds((16, tiles), F32)),
        4 * width * tiles * (pairs + 192),
        4 * tiles * width * 2,
    )(in_specs=[SMEM, SMEM] + [VMEM] * (6 + count))(
        local_bias, base, query, keys, values, *kv, left, right, adjacency.T
    )

    if inner:
        passed = []
        messages = []
        for g, size in enumerate(groups):
            at_one = place == 1
            onward = jnp.where(at_one, from_left[g], from_right[g])
            other = jnp.where(at_one, from_right[g], from_left[g])
            passed.append(move(onward, [(1, 2), (2, 1)]))
            message = call(
                functools.partial(guest_kernel, size, scale),
                sds((size * HEAD + 16, tiles), BF16),
                4 * size * HEAD * tiles * 3 * pairs,
                8 * tiles * size * HEAD * 2,
            )(in_specs=[SMEM] + [VMEM] * 4)(active, guest_q[g], kv[g], other, passed[g])
            messages.append(move(message, [(1, 0), (2, 3)]))
        shards = []
        for g in range(count):
            shards += [from_left[g], from_right[g], passed[g]]
        far, far_lse = call(
            functools.partial(far_kernel, groups, 3, scale),
            (sds((width, tiles), BF16), sds((16, tiles), F32)),
            4 * width * tiles * 3 * pairs,
            8 * tiles * width * 2,
        )(in_specs=[SMEM] + [VMEM] * (4 * count))(active, *q, *shards)
    else:
        active = jnp.ones((1,), jnp.int32)
        order = ((place + 1 + jnp.arange(ring - 1, dtype=jnp.int32)) % ring).astype(jnp.int32)
        messages, parts = [], []
        for g, size in enumerate(groups):
            parts.append(
                call(
                    functools.partial(ring_kernel, size, scale),
                    (sds((size * HEAD, tiles), BF16), sds((16, tiles), F32)),
                    4 * size * HEAD * tiles * ring * pairs,
                    2 * ring * pairs * size * HEAD * 2,
                    56,
                )(in_specs=[SMEM, VMEM, VMEM])(order, q[g], lax.all_gather(kv[g], "seq"))
            )
        far = jnp.concatenate([part[0] for part in parts], axis=0)
        far_lse = jnp.concatenate(
            [part[1][:size] for part, size in zip(parts, groups)]
            + [jnp.zeros((16 - heads, tiles), F32)],
            axis=0,
        )

    embed, tile_loss, sums = pl.pallas_call(
        functools.partial(final_kernel, groups),
        out_shape=(sds((tiles, width), BF16), sds((1, tiles), F32), sds((16, HEAD), F32)),
        in_specs=[SMEM, SMEM] + [VMEM] * (6 + len(messages)),
        scratch_shapes=[pltpu.VMEM((width, tiles), BF16), pltpu.VMEM((tiles, width), F32)],
        compiler_params=pltpu.CompilerParams(vmem_limit_bytes=32 * 1024 * 1024),
        cost_estimate=pl.CostEstimate(
            flops=2 * tiles * width * width, bytes_accessed=2 * width * width, transcendentals=0
        ),
    )(active, tissue, near, near_lse, far, far_lse, *messages, w_out, teacher_tile)

    reach = 1
    received = None
    if ring & (ring - 1) == 0:
        while reach < ring:
            if received is not None:
                sums = sums + received
            received = move(sums, [(i, i ^ reach) for i in range(ring)])
            reach *= 2
    else:
        received = lax.psum(sums, "seq") - sums
    slide, loss = pl.pallas_call(
        slide_kernel,
        out_shape=(sds((width // HEAD, HEAD), F32), sds((1,), F32)),
        in_specs=[VMEM] * 3,
        out_specs=(VMEM, SMEM),
    )(sums, received, teacher_slide.reshape(width // HEAD, HEAD))
    return embed, tile_loss.reshape(tiles), slide.reshape(width), loss


def solution(mesh):
    tiled = P(("dp", "seq"), None)
    return jax.shard_map(
        per_device,
        mesh=mesh,
        in_specs=(
            tiled,
            tiled,
            tiled,
            tiled,
            P(("dp", "seq")),
            P(),
            P(),
            P(),
            tiled,
            P("dp"),
        ),
        out_specs=(tiled, P(("dp", "seq")), P("dp"), P("dp")),
        check_vma=False,
    )
```
